256 devices in a mesh: row: 16 (over z, core), col: 16 (over y, x).
Axes of the slice: x: 4, y: 4, z: 8, core: 2. Of those that a mesh axis runs over, the one named last changes fastest.
Arguments:
- start_basis: float32 [32, 131072], P(None, ('row', 'col')), may hold values from -6 to 6
- degrees: float32 [131072], P(('row', 'col')), may hold values from 0.5 to 1.5
- tiles: float32 [8192, 256, 256], P(('row', 'col')), may hold values from -0.046875 to 0.046875
- tile_rows: int32 [16, 512], P('row', 'col'), may hold values from 0 to 31, as said below
- tile_cols: int32 [16, 512], P('row', 'col'), may hold values from 0 to 31
- counts: int32 [16, 16], P('row', 'col'), may hold values from 1 to 31, as said below
Outputs:
- basis: float32 [32, 131072], P(None, ('row', 'col'))
- projected: float32 [32, 32], replicated
The draws below stay inside these ranges and needn't reach their ends.
Inputs may be any that keep to these rules, and one draw needn't show every extreme that they name: `tile_rows`: the 32 (row, column) pairs of one device are distinct. counts[r, c] + counts[r', c] <= 32 where r' differs from r by 8; equality holds in column 0.
All inputs are finite; a program needn't handle non-finite values.
Results may differ from the reference program's by a relative error of at most 0.0003.
Values sent between devices are 32-bit elements; how exact they have to be, the bound alone decides.
A program may use at most 64 MiB of HBM per device.

```python
import jax
import jax.numpy as jnp
from jax import lax

BS = 256
SUBSPACE = 32
BLK_DEV = 2
TMAX = 32
DEGREE = 3
NVERT = 131072
N_ROW = 16
N_COL = 16


def tile_grid(key):
    cells = N_COL * BLK_DEV * N_ROW * BLK_DEV

    def one_device(index):
        return jax.random.permutation(jax.random.fold_in(key, 1000 + index), cells)[:TMAX]
    picked = jax.vmap(one_device)(jnp.arange(N_ROW * N_COL, dtype=jnp.int32))
    return picked.reshape(N_ROW, N_COL * TMAX)


def draw_tile_rows(key, part):
    return (tile_grid(key) // (N_ROW * BLK_DEV)).astype(jnp.int32)


def draw_tile_cols(key, part):
    return (tile_grid(key) % (N_ROW * BLK_DEV)).astype(jnp.int32)


def draw_counts(key, part):
    pair_rows = N_ROW // 2
    heavy_first = jax.random.randint(jax.random.fold_in(key, 1), (pair_rows, N_COL), 0, 2)
    heavy_load = jax.random.randint(jax.random.fold_in(key, 2), (pair_rows, N_COL), 3 * TMAX // 4, TMAX)
    row_index = jnp.arange(pair_rows, dtype=jnp.int32)[:, None]
    column_index = jnp.arange(N_COL, dtype=jnp.int32)[None, :]
    corner = (row_index == 0) & (column_index == 0)
    heavy_load = jnp.where(corner, TMAX - 1, heavy_load)
    light_load = jax.random.randint(jax.random.fold_in(key, 3), (pair_rows, N_COL), 1, TMAX - heavy_load + 1)
    light_load = jnp.where(column_index == 0, TMAX - heavy_load, jnp.where(column_index == 1, 1, light_load))
    upper_half = jnp.where(heavy_first == 1, heavy_load, light_load)
    bottom = jnp.where(heavy_first == 1, light_load, heavy_load)
    return jnp.concatenate([upper_half, bottom], 0).astype(jnp.int32)


def block_scale(stream_key, shape, split, low, top_value):
    factor_of, own = 1.0, jax.random.fold_in(stream_key, 6)
    for dim, blocks in split:
        draws = jnp.exp(jax.random.uniform(jax.random.fold_in(own, dim), (blocks,), jnp.float32, low / len(split), top_value / len(split)))
        factor_of = factor_of * jnp.repeat(draws, shape[dim] // blocks).reshape([-1 if axis == dim else 1 for axis in range(len(shape))])
    return factor_of


def normal_values(stream_key, extent, spread, reach, split=(), held_as=jnp.bfloat16):
    array = spread * jax.random.normal(stream_key, extent, jnp.float32)
    if split:
        array = array * block_scale(stream_key, extent, split, -0.22, 0.18)
    return jnp.clip(array, -reach, reach).astype(held_as)


def setup_inputs(seed: int = 0) -> dict:
    splits = jax.random.split(jax.random.key(seed), 7)
    start_basis = normal_values(splits[0], (SUBSPACE, NVERT), 1.0, 6.0, ((1, 256),), jnp.float32)
    degrees = jnp.clip(0.5 + 1.0 * jax.random.uniform(splits[1], (NVERT,), jnp.float32) ** block_scale(splits[1], (NVERT,), ((0, 256),), -0.2, 0.2), 0.5, 1.5)
    tiles = normal_values(splits[2], (N_ROW * N_COL * TMAX, BS, BS), (4 * TMAX * BS // BLK_DEV) ** -0.5, 0.046875, ((0, 256),), jnp.float32)
    tile_rows = draw_tile_rows(jax.random.fold_in(splits[6], 71), 0)
    tile_cols = draw_tile_cols(jax.random.fold_in(splits[6], 71), 0)
    counts = draw_counts(jax.random.fold_in(splits[6], 71), 0)
    return {"start_basis": start_basis, "degrees": degrees, "tiles": tiles, "tile_rows": tile_rows, "tile_cols": tile_cols, "counts": counts}


center_shift = 1.0
spread_radius = 1.4
group_width = 8

def operator_apply(vectors, degrees, tiles, tile_rows, tile_cols, counts):
    block_total = N_ROW * N_COL * BLK_DEV
    blocks = vectors.reshape(SUBSPACE, block_total, BS)

    def per_device(total, device):
        row_index = device // N_COL
        col_index = device % N_COL
        own_tiles = lax.dynamic_slice_in_dim(tiles, device * TMAX, TMAX, 0)
        row_local = lax.dynamic_slice_in_dim(tile_rows[row_index], col_index * TMAX, TMAX, 0)
        col_local = lax.dynamic_slice_in_dim(tile_cols[row_index], col_index * TMAX, TMAX, 0)
        row_global = ((row_index * N_COL + row_local // BLK_DEV) * BLK_DEV + row_local % BLK_DEV).astype(jnp.int32)
        col_global = ((col_local // BLK_DEV * N_COL + col_index) * BLK_DEV + col_local % BLK_DEV).astype(jnp.int32)
        live = counts[row_index, col_index]

        def add_group(index, inner):
            start = (index * group_width).astype(jnp.int32)
            group_tiles = lax.dynamic_slice_in_dim(own_tiles, start, group_width, 0)
            group_rows = lax.dynamic_slice_in_dim(row_global, start, group_width, 0)
            group_cols = lax.dynamic_slice_in_dim(col_global, start, group_width, 0)
            picked = jnp.take(blocks, group_cols, axis=1)
            product = jnp.einsum('kgj,gij->kgi', picked, group_tiles, precision=lax.Precision.HIGHEST)
            valid = (start + jnp.arange(group_width, dtype=jnp.int32) < live).astype(jnp.float32)
            return inner.at[:, group_rows, :].add(product * valid[None, :, None])
        total = lax.fori_loop(0, (live + group_width - 1) // group_width, add_group, total)
        return (total, None)
    initial = jnp.zeros((SUBSPACE, block_total, BS), jnp.float32)
    total, unused = lax.scan(per_device, initial, jnp.arange(N_ROW * N_COL, dtype=jnp.int32))
    return degrees[None, :] * vectors - total.reshape(SUBSPACE, block_total * BS)

def reference(start_basis, degrees, tiles, tile_rows, tile_cols, counts):
    nverts = N_ROW * N_COL * BLK_DEV * BS

    def shifted(vectors):
        image = operator_apply(vectors, degrees, tiles, tile_rows, tile_cols, counts)
        return (image - center_shift * vectors) / spread_radius
    previous = start_basis
    current = shifted(start_basis)
    for level in range(DEGREE - 1):
        following = 2.0 * shifted(current) - previous
        previous, current = (current, following)
    gram_matrix = jnp.einsum('kn,mn->km', current, current, precision=lax.Precision.HIGHEST) / nverts
    factor = jnp.linalg.cholesky(gram_matrix)
    basis = jax.scipy.linalg.solve_triangular(factor, current, lower=True)
    image = operator_apply(basis, degrees, tiles, tile_rows, tile_cols, counts)
    moment = jnp.einsum('kn,mn->km', basis, image, precision=lax.Precision.HIGHEST) / nverts
    projected = 0.5 * (moment + moment.T)
    return (basis, projected)
```

```python
import jax
import jax.numpy as jnp
from jax import lax
from jax.experimental import pallas as pl
from jax.experimental.pallas import tpu as pltpu
from jax.sharding import PartitionSpec as P

BS = 256
SUB = 32
TMAX = 32
N_ROW = 16
N_COL = 16
SIDE = 4
Z = 8
NVERT = 131072

CENTER = 1.0
INV_RADIUS = 1.0 / 1.4

F32 = jnp.float32
BF16 = jnp.bfloat16
HIGH = lax.Precision.HIGHEST
NT = (((1,), (1,)), ((), ()))
NN = (((1,), (0,)), ((), ()))


def split(value):
    high = value.astype(BF16)
    return high, (value - high.astype(F32)).astype(BF16)


def pack(square):
    return jnp.concatenate([square[8 * s : 8 * s + 8, :] for s in range(4)], axis=1)


def unpack(flat):
    return jnp.concatenate([flat[:, 32 * s : 32 * s + 32] for s in range(4)], axis=0)


def flip_low(p):
    return p + 1 - 2 * lax.rem(p, 2)


def flip_high(p):
    return lax.rem(p + 3 + 2 * lax.rem(p, 2), SIDE)


def inverse_factor(gram):
    rows = lax.broadcasted_iota(jnp.int32, (32, 128), 0)
    lanes = lax.broadcasted_iota(jnp.int32, (32, 128), 1)
    eye = (rows[:, :32] == lanes[:, :32]).astype(F32)
    table = jnp.concatenate([eye, gram, jnp.zeros((32, 64), F32)], axis=1)
    for j in range(32):
        pivot = table[j : j + 1, 32 + j : 33 + j]
        guess = lax.rsqrt(pivot)
        inv = guess * (1.5 - 0.5 * pivot * guess * guess)
        row = table[j : j + 1, :] * inv
        col = table[:, 32 + j : 33 + j] * inv
        table = jnp.where(rows == j, row, jnp.where(rows > j, table - col * row, table))
    return table[:, :32]


def kernel(index_ref, x_ref, deg_ref, tiles_ref, basis_ref, proj_ref,
           stage, whi, wlo, xg, xs, run, part, land, fcol, fstack, red,
           tile_sem, z_send, z_recv, p_send, p_recv, rs_send, rs_recv,
           fc_send, fc_recv, ar_send, ar_recv):
    r = lax.axis_index("row")
    c = lax.axis_index("col")
    z = r // 2
    core = lax.rem(r, 2)
    cx = lax.rem(c, SIDE)
    cy = c // SIDE

    for t in range(8):
        pltpu.make_async_copy(tiles_ref.at[pl.ds(4 * t, 4)], stage.at[pl.ds(4 * t, 4)], tile_sem.at[t]).start()

    barrier = pltpu.get_barrier_semaphore()
    for q in range(1, 16):
        pl.semaphore_signal(barrier, inc=1, device_id={"row": lax.rem(r + q, 16)})
        pl.semaphore_signal(barrier, inc=1, device_id={"col": lax.rem(c + q, 16)})

    def slot_of(distance):
        return lax.rem(z - distance + Z, Z) * 2 + core

    def z_copy(a, d, hop, h):
        slot = slot_of((hop - 1) * (1 if d == 0 else -1))
        target = lax.rem(z + (1 if d == 0 else Z - 1), Z) * 2 + core
        piece = xg.at[a, slot, h]
        return pltpu.make_async_remote_copy(
            src_ref=piece, dst_ref=piece,
            send_sem=z_send.at[a, d, hop - 1, h], recv_sem=z_recv.at[a, d, hop - 1, h],
            device_id={"row": target})

    def p_copy(a, k, h):
        distance = k if k <= 3 else (4 if k == 7 else 3 - k)
        piece = xg.at[a, slot_of(distance), h]
        return pltpu.make_async_remote_copy(
            src_ref=piece, dst_ref=piece,
            send_sem=p_send.at[a, k, h], recv_sem=p_recv.at[a, k, h],
            device_id={"row": r + 1 - 2 * core})

    def convert(a, slot, h):
        high, low = split(xg[a, slot, h])
        xs[slot * 2 + h, 0:32, :] = high
        xs[slot * 2 + h, 32:64, :] = low

    def exists(d, hop, h):
        return hop <= 3 or (hop == 4 and h == d)

    def gather_start(a):
        for h in range(2):
            for d in range(2):
                z_copy(a, d, 1, h).start()
            p_copy(a, 0, h).start()
        for h in range(2):
            convert(a, r, h)

    def gather_hop(a, hop):
        for h in range(2):
            for d in range(2):
                if exists(d, hop, h):
                    z_copy(a, d, hop, h).wait_recv()
                    if exists(d, hop + 1, h):
                        z_copy(a, d, hop + 1, h).start()
                    k = 7 if hop == 4 else hop + 3 * d
                    p_copy(a, k, h).start()
                    convert(a, slot_of(hop * (1 if d == 0 else -1)), h)

    def gather_end(a):
        for k in range(8):
            distance = k if k <= 3 else (4 if k == 7 else 3 - k)
            slot = slot_of(distance) + 1 - 2 * core
            for h in range(2):
                p_copy(a, k, h).wait_recv()
                convert(a, slot, h)
        for hop in range(1, 5):
            for h in range(2):
                for d in range(2):
                    if exists(d, hop, h):
                        z_copy(a, d, hop, h).wait_send()
        for k in range(8):
            for h in range(2):
                p_copy(a, k, h).wait_send()

    def products():
        def one(t):
            j = index_ref[0, t]
            both = lax.dot_general(xs[j], whi[t], NN, preferred_element_type=F32)
            cross = lax.dot_general(xs[j, 0:32, :], wlo[t], NN, preferred_element_type=F32)
            run[t] = (both[0:32] + both[32:64]) + cross + run[index_ref[1, t]]

        def group(g, carry):
            for u in range(4):
                one(g * 4 + u)
            return carry
        lax.fori_loop(0, TMAX // 4, group, 0)

    def split_tiles(t):
        def one(i, carry):
            high, low = split(stage[i].T)
            whi[i] = high
            wlo[i] = low
            return carry
        lax.fori_loop(4 * t, 4 * t + 4, one, 0)

    flips = (
        {"col": cy * SIDE + flip_low(cx)},
        {"col": cy * SIDE + flip_high(cx)},
        {"col": flip_low(cy) * SIDE + cx},
        {"col": flip_high(cy) * SIDE + cx},
    )

    def owner(bits):
        px, py = cx, cy
        if bits[0]:
            px = flip_low(px)
        if bits[1]:
            px = flip_high(px)
        if bits[2]:
            py = flip_low(py)
        if bits[3]:
            py = flip_high(py)
        return py * SIDE + px

    def place(s, bits):
        return sum(bits[(s + step) % 4] << (3 - step) for step in range(4))

    combos = [tuple((n >> k) & 1 for k in range(4)) for n in range(16)]

    def scatter_copy(a, s, step):
        half = 8 >> step
        start = (0, 8, 12, 14)[step]
        return pltpu.make_async_remote_copy(
            src_ref=part.at[a, s, pl.ds(half, half)],
            dst_ref=land.at[a, s, pl.ds(start, half)],
            send_sem=rs_send.at[a, s, step], recv_sem=rs_recv.at[a, s, step],
            device_id=flips[(s + step) % 4])

    def scatter(a):
        for bits in combos:
            dest = owner(bits)
            for h in range(2):
                block = run[index_ref[2, 2 * dest + h]]
                for s in range(4):
                    part[a, s, place(s, bits), h] = block[8 * s : 8 * s + 8, :]
        for s in range(4):
            scatter_copy(a, s, 0).start()
        for step in range(4):
            half = 8 >> step
            start = (0, 8, 12, 14)[step]
            for s in range(4):
                scatter_copy(a, s, step).wait_recv()
                part[a, s, 0:half] = part[a, s, 0:half] + land[a, s, start : start + half]
                if step < 3:
                    scatter_copy(a, s, step + 1).start()

    def scatter_end(a):
        for s in range(4):
            for step in range(4):
                scatter_copy(a, s, step).wait_send()

    def fcol_copy(s, step):
        size = 1 << step
        return pltpu.make_async_remote_copy(
            src_ref=fcol.at[s, pl.ds(0, size)],
            dst_ref=fcol.at[s, pl.ds(size, size)],
            send_sem=fc_send.at[s, step], recv_sem=fc_recv.at[s, step],
            device_id=flips[(s + 3 - step) % 4])

    def ar_copy(w, level, q):
        if level == 0:
            mine, peer = r, {"row": lax.rem(r + q, 16)}
        else:
            mine, peer = c, {"col": lax.rem(c + q, 16)}
        piece = red.at[w, level, mine]
        return pltpu.make_async_remote_copy(
            src_ref=piece, dst_ref=piece,
            send_sem=ar_send.at[w, level, q], recv_sem=ar_recv.at[w, level, q],
            device_id=peer)

    def ar_start(w, level, value):
        red[w, level, r if level == 0 else c] = value
        for q in range(1, 16):
            ar_copy(w, level, q).start()

    def ar_end(w, level):
        for q in range(1, 16):
            ar_copy(w, level, q).wait_recv()
        total = red[w, level, 0]
        for q in range(1, 16):
            total = total + red[w, level, q]
        for q in range(1, 16):
            ar_copy(w, level, q).wait_send()
        return total

    for h in range(2):
        xg[0, r, h] = x_ref[:, BS * h : BS * h + BS]
    run[TMAX] = jnp.zeros((SUB, BS), F32)
    pl.semaphore_wait(barrier, 30)
    gather_start(0)
    for hop in range(1, 5):
        for t in range(2 * hop - 2, 2 * hop):
            pltpu.make_async_copy(tiles_ref.at[pl.ds(4 * t, 4)], stage.at[pl.ds(4 * t, 4)], tile_sem.at[t]).wait()
            split_tiles(t)
        gather_hop(0, hop)
    gather_end(0)

    for a in range(3):
        if a > 0:
            gather_start(a)
            for hop in range(1, 5):
                gather_hop(a, hop)
            gather_end(a)
        products()
        scatter(a)
        for h in range(2):
            gap = deg_ref[0:1, BS * h : BS * h + BS] - CENTER
            for s in range(4):
                rows = slice(8 * s, 8 * s + 8)
                now = xg[a, r, h, rows, :]
                image = (gap * now - part[a, s, 0, h]) * INV_RADIUS
                if a > 0:
                    image = 2.0 * image - xg[a - 1, r, h, rows, :]
                xg[a + 1, r, h, rows, :] = image
                if a == 2:
                    fcol[s, 0, h] = image
        scatter_end(a)

    gather_start(3)
    for s in range(4):
        fcol_copy(s, 0).start()
    gram = jnp.zeros((SUB, SUB), F32)
    shift = jnp.zeros((SUB, SUB), F32)
    for h in range(2):
        own = xg[3, r, h]
        gram = gram + lax.dot_general(own, own, NT, precision=HIGH, preferred_element_type=F32)
        shift = shift + lax.dot_general(own, own * deg_ref[0:1, BS * h : BS * h + BS], NT, precision=HIGH,
                                        preferred_element_type=F32)
    ar_start(0, 0, pack(gram))

    def column_step(step):
        for s in range(4):
            fcol_copy(s, step).wait_recv()
            if step < 3:
                fcol_copy(s, step + 1).start()

    gather_hop(3, 1)
    column_step(0)
    gather_hop(3, 2)
    column_step(1)
    ar_start(0, 1, ar_end(0, 0))
    gather_hop(3, 3)
    column_step(2)
    gather_hop(3, 4)
    gather_end(3)
    products()
    column_step(3)
    for s in range(4):
        for step in range(4):
            fcol_copy(s, step).wait_send()
    for bits in combos:
        dest = owner(bits)
        for h in range(2):
            for s in range(4):
                piece = fcol[s, place(s, bits), h]
                fstack[2 * dest + h, 8 * s : 8 * s + 8, :] = piece

    def pair(i, acc):
        left = jnp.concatenate(split(fstack[i]), axis=0)
        right = jnp.concatenate(split(run[index_ref[2, i]]), axis=0)
        return acc + lax.dot_general(left, right, NT, preferred_element_type=F32)

    quad = lax.fori_loop(0, 2 * N_COL, pair, jnp.zeros((2 * SUB, 2 * SUB), F32))
    coupling = quad[0:32, 0:32] + quad[0:32, 32:64] + quad[32:64, 0:32] + quad[32:64, 32:64]
    ar_start(1, 0, pack(shift - coupling))
    total_gram = unpack(ar_end(0, 1)) * (1.0 / NVERT)
    inv = inverse_factor(total_gram)
    for h in range(2):
        basis_ref[:, BS * h : BS * h + BS] = lax.dot_general(
            inv, xg[3, r, h], NN, precision=HIGH, preferred_element_type=F32)
    ar_start(1, 1, ar_end(1, 0))
    moment = unpack(ar_end(1, 1)) * (1.0 / NVERT)
    half = lax.dot_general(inv, moment, NN, precision=HIGH, preferred_element_type=F32)
    full = lax.dot_general(half, inv, NT, precision=HIGH, preferred_element_type=F32)
    proj_ref[...] = 0.5 * (full + full.T)


def body(start_basis, degrees, tiles, tile_rows, tile_cols, counts):
    rows = tile_rows[0]
    live = counts[0, 0]
    slot = jnp.arange(TMAX, dtype=jnp.int32)
    earlier = (rows[:, None] == rows[None, :]) & (slot[None, :] < slot[:, None])
    before = jnp.max(jnp.where(earlier, slot[None, :], -1), axis=1)
    before = jnp.where(before < 0, TMAX, before)
    ends = (rows[None, :] == slot[:, None]) & (slot[None, :] < live)
    last = jnp.max(jnp.where(ends, slot[None, :], -1), axis=1)
    last = jnp.where(last < 0, TMAX, last)
    index = jnp.stack([tile_cols[0], before, last])
    vmem = pl.BlockSpec(memory_space=pltpu.VMEM)
    dma = pltpu.SemaphoreType.DMA
    return pl.pallas_call(
        kernel,
        out_shape=(jax.ShapeDtypeStruct((SUB, 2 * BS), F32), jax.ShapeDtypeStruct((SUB, SUB), F32)),
        in_specs=[pl.BlockSpec(memory_space=pltpu.SMEM), vmem, vmem, pl.BlockSpec(memory_space=pl.ANY)],
        out_specs=(vmem, vmem),
        scratch_shapes=[
            pltpu.VMEM((TMAX, BS, BS), F32),
            pltpu.VMEM((TMAX, BS, BS), BF16),
            pltpu.VMEM((TMAX, BS, BS), BF16),
            pltpu.VMEM((4, N_ROW, 2, SUB, BS), F32),
            pltpu.VMEM((2 * N_ROW, 2 * SUB, BS), BF16),
            pltpu.VMEM((TMAX + 1, SUB, BS), F32),
            pltpu.VMEM((3, 4, 16, 2, 8, BS), F32),
            pltpu.VMEM((3, 4, 15, 2, 8, BS), F32),
            pltpu.VMEM((4, 16, 2, 8, BS), F32),
            pltpu.VMEM((2 * N_COL, SUB, BS), F32),
            pltpu.VMEM((2, 2, 16, 8, 128), F32),
            dma((8,)),
            dma((4, 2, 4, 2)), dma((4, 2, 4, 2)),
            dma((4, 8, 2)), dma((4, 8, 2)),
            dma((3, 4, 4)), dma((3, 4, 4)),
            dma((4, 4)), dma((4, 4)),
            dma((2, 2, 16)), dma((2, 2, 16)),
        ],
        compiler_params=pltpu.CompilerParams(collective_id=0, has_side_effects=True, vmem_limit_bytes=56 << 20),
        name="subspace_step",
    )(index, start_basis, degrees.reshape(1, -1), tiles)


def solution(mesh):
    return jax.shard_map(
        body,
        mesh=mesh,
        in_specs=(
            P(None, ("row", "col")),
            P(("row", "col")),
            P(("row", "col"), None, None),
            P("row", "col"),
            P("row", "col"),
            P("row", "col"),
        ),
        out_specs=(P(None, ("row", "col")), P()),
        check_vma=False,
    )
```

```python
import jax
import jax.numpy as jnp
from jax import lax
from jax.experimental import pallas as pl
from jax.experimental.pallas import tpu as pltpu
from jax.sharding import PartitionSpec as P

BS = 256
SUB = 32
TMAX = 32
N_ROW = 16
N_COL = 16
SIDE = 4
Z = 8
NVERT = 131072

CENTER = 1.0
INV_RADIUS = 1.0 / 1.4

F32 = jnp.float32
BF16 = jnp.bfloat16
HIGH = lax.Precision.HIGHEST
NT = (((1,), (1,)), ((), ()))
NN = (((1,), (0,)), ((), ()))


def split(value):
    high = value.astype(BF16)
    return high, (value - high.astype(F32)).astype(BF16)


def pack(square):
    return jnp.concatenate([square[8 * s : 8 * s + 8, :] for s in range(4)], axis=1)


def unpack(flat):
    return jnp.concatenate([flat[:, 32 * s : 32 * s + 32] for s in range(4)], axis=0)


def flip_low(p):
    return p + 1 - 2 * lax.rem(p, 2)


def flip_high(p):
    return lax.rem(p + 3 + 2 * lax.rem(p, 2), SIDE)


def inverse_factor(gram):
    rows = lax.broadcasted_iota(jnp.int32, (32, 128), 0)
    lanes = lax.broadcasted_iota(jnp.int32, (32, 128), 1)
    eye = (rows[:, :32] == lanes[:, :32]).astype(F32)
    table = jnp.concatenate([eye, gram, jnp.zeros((32, 64), F32)], axis=1)
    for j in range(32):
        pivot = table[j : j + 1, 32 + j : 33 + j]
        guess = lax.rsqrt(pivot)
        inv = guess * (1.5 - 0.5 * pivot * guess * guess)
        row = table[j : j + 1, :] * inv
        col = table[:, 32 + j : 33 + j] * inv
        table = jnp.where(rows == j, row, jnp.where(rows > j, table - col * row, table))
    return table[:, :32]


def kernel(index_ref, x_ref, deg_ref, tiles_ref, basis_ref, proj_ref,
           stage, whi, wlo, xg, xs, run, part, land, fcol, fstack, red,
           tile_sem, z_send, z_recv, p_send, p_recv, rs_send, rs_recv,
           fc_send, fc_recv, ar_send, ar_recv):
    r = lax.axis_index("row")
    c = lax.axis_index("col")
    z = r // 2
    core = lax.rem(r, 2)
    cx = lax.rem(c, SIDE)
    cy = c // SIDE

    for t in range(8):
        pltpu.make_async_copy(tiles_ref.at[pl.ds(4 * t, 4)], stage.at[pl.ds(4 * t, 4)], tile_sem.at[t]).start()

    barrier = pltpu.get_barrier_semaphore()
    for q in range(1, 16):
        pl.semaphore_signal(barrier, inc=1, device_id={"row": lax.rem(r + q, 16)})
        pl.semaphore_signal(barrier, inc=1, device_id={"col": lax.rem(c + q, 16)})

    def slot_of(distance):
        return lax.rem(z - distance + Z, Z) * 2 + core

    def z_copy(a, d, hop, h):
        slot = slot_of((hop - 1) * (1 if d == 0 else -1))
        target = lax.rem(z + (1 if d == 0 else Z - 1), Z) * 2 + core
        piece = xg.at[a, slot, h]
        return pltpu.make_async_remote_copy(
            src_ref=piece, dst_ref=piece,
            send_sem=z_send.at[a, d, hop - 1, h], recv_sem=z_recv.at[a, d, hop - 1, h],
            device_id={"row": target})

    def p_copy(a, k, h):
        distance = k if k <= 3 else (4 if k == 7 else 3 - k)
        piece = xg.at[a, slot_of(distance), h]
        return pltpu.make_async_remote_copy(
            src_ref=piece, dst_ref=piece,
            send_sem=p_send.at[a, k, h], recv_sem=p_recv.at[a, k, h],
            device_id={"row": r + 1 - 2 * core})

    def convert(a, slot, h):
        high, low = split(xg[a, slot, h])
        xs[slot * 2 + h, 0:32, :] = high
        xs[slot * 2 + h, 32:64, :] = low

    def exists(d, hop, h):
        return hop <= 3 or (hop == 4 and h == d)

    def gather_send(a, h):
        for d in range(2):
            z_copy(a, d, 1, h).start()
        p_copy(a, 0, h).start()

    def gather_hop(a, hop):
        for h in range(2):
            for d in range(2):
                if exists(d, hop, h):
                    z_copy(a, d, hop, h).wait_recv()
                    if exists(d, hop + 1, h):
                        z_copy(a, d, hop + 1, h).start()
                    k = 7 if hop == 4 else hop + 3 * d
                    p_copy(a, k, h).start()
                    convert(a, slot_of(hop * (1 if d == 0 else -1)), h)

    def gather_end(a):
        for k in range(8):
            distance = k if k <= 3 else (4 if k == 7 else 3 - k)
            slot = slot_of(distance) + 1 - 2 * core
            for h in range(2):
                p_copy(a, k, h).wait_recv()
                convert(a, slot, h)
        for hop in range(1, 5):
            for h in range(2):
                for d in range(2):
                    if exists(d, hop, h):
                        z_copy(a, d, hop, h).wait_send()
        for k in range(8):
            for h in range(2):
                p_copy(a, k, h).wait_send()

    def products():
        def one(t):
            j = index_ref[0, t]
            both = lax.dot_general(xs[j], whi[t], NN, preferred_element_type=F32)
            cross = lax.dot_general(xs[j, 0:32, :], wlo[t], NN, preferred_element_type=F32)
            run[t] = (both[0:32] + both[32:64]) + cross + run[index_ref[1, t]]

        def group(g, carry):
            for u in range(4):
                one(g * 4 + u)
            return carry
        lax.fori_loop(0, TMAX // 4, group, 0)

    def split_tiles(t):
        def one(i, carry):
            high, low = split(stage[i].T)
            whi[i] = high
            wlo[i] = low
            return carry
        lax.fori_loop(4 * t, 4 * t + 4, one, 0)

    flips = (
        {"col": cy * SIDE + flip_low(cx)},
        {"col": cy * SIDE + flip_high(cx)},
        {"col": flip_low(cy) * SIDE + cx},
        {"col": flip_high(cy) * SIDE + cx},
    )

    def owner(bits):
        px, py = cx, cy
        if bits[0]:
            px = flip_low(px)
        if bits[1]:
            px = flip_high(px)
        if bits[2]:
            py = flip_low(py)
        if bits[3]:
            py = flip_high(py)
        return py * SIDE + px

    def place(s, bits):
        return sum(bits[(s + step) % 4] << (3 - step) for step in range(4))

    combos = [tuple((n >> k) & 1 for k in range(4)) for n in range(16)]

    def pair_bits(s, steps):
        bits = [0, 0, 0, 0]
        for step in steps:
            bits[(s + step) % 4] = 1
        return tuple(bits)

    def scatter_copy(a, s, h, n):
        size = (8, 4, 1, 1, 1)[n]
        first = (8, 4, 2, 1, 3)[n]
        start = (0, 8, 12, 13, 14)[n]
        steps = ((0,), (1,), (2,), (3,), (2, 3))[n]
        return pltpu.make_async_remote_copy(
            src_ref=part.at[a, s, h, pl.ds(first, size)],
            dst_ref=land.at[a, s, h, pl.ds(start, size)],
            send_sem=rs_send.at[a, s, h, n], recv_sem=rs_recv.at[a, s, h, n],
            device_id={"col": owner(pair_bits(s, steps))})

    def scatter(a):
        for h in range(2):
            for bits in combos:
                block = run[index_ref[2, 2 * owner(bits) + h]]
                for s in range(4):
                    part[a, s, h, place(s, bits)] = block[8 * s : 8 * s + 8, :]
            for s in range(4):
                scatter_copy(a, s, h, 0).start()
        for step in range(2):
            half = 8 >> step
            start = (0, 8)[step]
            for h in range(2):
                for s in range(4):
                    scatter_copy(a, s, h, step).wait_recv()
                    part[a, s, h, 0:half] = part[a, s, h, 0:half] + land[a, s, h, start : start + half]
                    for n in ((1,), (4, 2, 3))[step]:
                        scatter_copy(a, s, h, n).start()

    def scatter_sum(a, s, h):
        for n in (2, 3, 4):
            scatter_copy(a, s, h, n).wait_recv()
        return (part[a, s, h, 0] + land[a, s, h, 12]) + (land[a, s, h, 13] + land[a, s, h, 14])

    def scatter_end(a):
        for s in range(4):
            for h in range(2):
                for n in range(5):
                    scatter_copy(a, s, h, n).wait_send()

    def fcol_copy(s, step):
        size = 1 << step
        return pltpu.make_async_remote_copy(
            src_ref=fcol.at[s, pl.ds(0, size)],
            dst_ref=fcol.at[s, pl.ds(size, size)],
            send_sem=fc_send.at[s, step], recv_sem=fc_recv.at[s, step],
            device_id=flips[(s + 3 - step) % 4])

    def ar_copy(w, level, q):
        if level == 0:
            mine, peer = r, {"row": lax.rem(r + q, 16)}
        else:
            mine, peer = c, {"col": lax.rem(c + q, 16)}
        piece = red.at[w, level, mine]
        return pltpu.make_async_remote_copy(
            src_ref=piece, dst_ref=piece,
            send_sem=ar_send.at[w, level, q], recv_sem=ar_recv.at[w, level, q],
            device_id=peer)

    def ar_start(w, level, value):
        red[w, level, r if level == 0 else c] = value
        for q in range(1, 16):
            ar_copy(w, level, q).start()

    def ar_end(w, level):
        for q in range(1, 16):
            ar_copy(w, level, q).wait_recv()
        total = red[w, level, 0]
        for q in range(1, 16):
            total = total + red[w, level, q]
        for q in range(1, 16):
            ar_copy(w, level, q).wait_send()
        return total

    for h in range(2):
        xg[0, r, h] = x_ref[:, BS * h : BS * h + BS]
    run[TMAX] = jnp.zeros((SUB, BS), F32)
    pl.semaphore_wait(barrier, 30)
    for h in range(2):
        gather_send(0, h)
    for h in range(2):
        convert(0, r, h)
    for hop in range(1, 5):
        for t in range(2 * hop - 2, 2 * hop):
            pltpu.make_async_copy(tiles_ref.at[pl.ds(4 * t, 4)], stage.at[pl.ds(4 * t, 4)], tile_sem.at[t]).wait()
            split_tiles(t)
        gather_hop(0, hop)
    gather_end(0)

    for a in range(3):
        if a > 0:
            for hop in range(1, 5):
                gather_hop(a, hop)
            gather_end(a)
        products()
        scatter(a)
        for h in range(2):
            gap = deg_ref[0:1, BS * h : BS * h + BS] - CENTER
            for s in range(4):
                rows = slice(8 * s, 8 * s + 8)
                now = xg[a, r, h, rows, :]
                image = (gap * now - scatter_sum(a, s, h)) * INV_RADIUS
                if a > 0:
                    image = 2.0 * image - xg[a - 1, r, h, rows, :]
                xg[a + 1, r, h, rows, :] = image
                if a == 2:
                    fcol[s, 0, h] = image
            gather_send(a + 1, h)
        for h in range(2):
            convert(a + 1, r, h)
        scatter_end(a)

    for s in range(4):
        fcol_copy(s, 0).start()
    gram = jnp.zeros((SUB, SUB), F32)
    shift = jnp.zeros((SUB, SUB), F32)
    for h in range(2):
        own = xg[3, r, h]
        gram = gram + lax.dot_general(own, own, NT, precision=HIGH, preferred_element_type=F32)
        shift = shift + lax.dot_general(own, own * deg_ref[0:1, BS * h : BS * h + BS], NT, precision=HIGH,
                                        preferred_element_type=F32)
    ar_start(0, 0, pack(gram))

    def column_step(step):
        for s in range(4):
            fcol_copy(s, step).wait_recv()
            if step < 3:
                fcol_copy(s, step + 1).start()

    gather_hop(3, 1)
    column_step(0)
    gather_hop(3, 2)
    column_step(1)
    ar_start(0, 1, ar_end(0, 0))
    gather_hop(3, 3)
    column_step(2)
    gather_hop(3, 4)
    gather_end(3)
    products()
    column_step(3)
    for s in range(4):
        for step in range(4):
            fcol_copy(s, step).wait_send()
    for bits in combos:
        dest = owner(bits)
        for h in range(2):
            for s in range(4):
                piece = fcol[s, place(s, bits), h]
                fstack[2 * dest + h, 8 * s : 8 * s + 8, :] = piece

    def pair(i):
        left = jnp.concatenate(split(fstack[i]), axis=0)
        right = jnp.concatenate(split(run[index_ref[2, i]]), axis=0)
        return lax.dot_general(left, right, NT, preferred_element_type=F32)

    def pairs(g, acc):
        return acc + ((pair(4 * g) + pair(4 * g + 1)) + (pair(4 * g + 2) + pair(4 * g + 3)))

    quad = lax.fori_loop(0, N_COL // 2, pairs, jnp.zeros((2 * SUB, 2 * SUB), F32))
    coupling = quad[0:32, 0:32] + quad[0:32, 32:64] + quad[32:64, 0:32] + quad[32:64, 32:64]
    ar_start(1, 0, pack(shift - coupling))
    total_gram = unpack(ar_end(0, 1)) * (1.0 / NVERT)
    inv = inverse_factor(total_gram)
    for h in range(2):
        basis_ref[:, BS * h : BS * h + BS] = lax.dot_general(
            inv, xg[3, r, h], NN, precision=HIGH, preferred_element_type=F32)
    ar_start(1, 1, ar_end(1, 0))
    moment = unpack(ar_end(1, 1)) * (1.0 / NVERT)
    half = lax.dot_general(inv, moment, NN, precision=HIGH, preferred_element_type=F32)
    full = lax.dot_general(half, inv, NT, precision=HIGH, preferred_element_type=F32)
    proj_ref[...] = 0.5 * (full + full.T)


def body(start_basis, degrees, tiles, tile_rows, tile_cols, counts):
    rows = tile_rows[0]
    live = counts[0, 0]
    slot = jnp.arange(TMAX, dtype=jnp.int32)
    earlier = (rows[:, None] == rows[None, :]) & (slot[None, :] < slot[:, None])
    before = jnp.max(jnp.where(earlier, slot[None, :], -1), axis=1)
    before = jnp.where(before < 0, TMAX, before)
    ends = (rows[None, :] == slot[:, None]) & (slot[None, :] < live)
    last = jnp.max(jnp.where(ends, slot[None, :], -1), axis=1)
    last = jnp.where(last < 0, TMAX, last)
    index = jnp.stack([tile_cols[0], before, last])
    vmem = pl.BlockSpec(memory_space=pltpu.VMEM)
    dma = pltpu.SemaphoreType.DMA
    return pl.pallas_call(
        kernel,
        out_shape=(jax.ShapeDtypeStruct((SUB, 2 * BS), F32), jax.ShapeDtypeStruct((SUB, SUB), F32)),
        in_specs=[pl.BlockSpec(memory_space=pltpu.SMEM), vmem, vmem, pl.BlockSpec(memory_space=pl.ANY)],
        out_specs=(vmem, vmem),
        scratch_shapes=[
            pltpu.VMEM((TMAX, BS, BS), F32),
            pltpu.VMEM((TMAX, BS, BS), BF16),
            pltpu.VMEM((TMAX, BS, BS), BF16),
            pltpu.VMEM((4, N_ROW, 2, SUB, BS), F32),
            pltpu.VMEM((2 * N_ROW, 2 * SUB, BS), BF16),
            pltpu.VMEM((TMAX + 1, SUB, BS), F32),
            pltpu.VMEM((3, 4, 2, 16, 8, BS), F32),
            pltpu.VMEM((3, 4, 2, 15, 8, BS), F32),
            pltpu.VMEM((4, 16, 2, 8, BS), F32),
            pltpu.VMEM((2 * N_COL, SUB, BS), F32),
            pltpu.VMEM((2, 2, 16, 8, 128), F32),
            dma((8,)),
            dma((4, 2, 4, 2)), dma((4, 2, 4, 2)),
            dma((4, 8, 2)), dma((4, 8, 2)),
            dma((3, 4, 2, 5)), dma((3, 4, 2, 5)),
            dma((4, 4)), dma((4, 4)),
            dma((2, 2, 16)), dma((2, 2, 16)),
        ],
        compiler_params=pltpu.CompilerParams(collective_id=0, has_side_effects=True, vmem_limit_bytes=56 << 20),
        name="subspace_step",
    )(index, start_basis, degrees.reshape(1, -1), tiles)


def solution(mesh):
    return jax.shard_map(
        body,
        mesh=mesh,
        in_specs=(
            P(None, ("row", "col")),
            P(("row", "col")),
            P(("row", "col"), None, None),
            P("row", "col"),
            P("row", "col"),
            P("row", "col"),
        ),
        out_specs=(P(None, ("row", "col")), P()),
        check_vma=False,
    )
```

```python
import jax
import jax.numpy as jnp
from jax import lax
from jax.experimental import pallas as pl
from jax.experimental.pallas import tpu as pltpu
from jax.sharding import PartitionSpec as P

BS = 256
SUB = 32
TMAX = 32
N_ROW = 16
N_COL = 16
SIDE = 4
Z = 8
NVERT = 131072

CENTER = 1.0
INV_RADIUS = 1.0 / 1.4

F32 = jnp.float32
BF16 = jnp.bfloat16
HIGH = lax.Precision.HIGHEST
NT = (((1,), (1,)), ((), ()))
NN = (((1,), (0,)), ((), ()))


def split(value):
    high = value.astype(BF16)
    return high, (value - high.astype(F32)).astype(BF16)


def pack(square):
    return jnp.concatenate([square[8 * s : 8 * s + 8, :] for s in range(4)], axis=1)


def unpack(flat):
    return jnp.concatenate([flat[:, 32 * s : 32 * s + 32] for s in range(4)], axis=0)


def flip_low(p):
    return p + 1 - 2 * lax.rem(p, 2)


def flip_high(p):
    return lax.rem(p + 3 + 2 * lax.rem(p, 2), SIDE)


def inverse_factor(gram):
    rows = lax.broadcasted_iota(jnp.int32, (32, 128), 0)
    lanes = lax.broadcasted_iota(jnp.int32, (32, 128), 1)
    eye = (rows[:, :32] == lanes[:, :32]).astype(F32)
    table = jnp.concatenate([eye, gram, jnp.zeros((32, 64), F32)], axis=1)
    for j in range(32):
        pivot = table[j : j + 1, 32 + j : 33 + j]
        guess = lax.rsqrt(pivot)
        inv = guess * (1.5 - 0.5 * pivot * guess * guess)
        row = table[j : j + 1, :] * inv
        col = table[:, 32 + j : 33 + j] * inv
        table = jnp.where(rows == j, row, jnp.where(rows > j, table - col * row, table))
    return table[:, :32]


def kernel(index_ref, x_ref, deg_ref, tiles_ref, basis_ref, proj_ref,
           stage, whi, wlo, xg, xs, run, part, land, fcol, red,
           tile_sem, z_send, z_recv, p_send, p_recv, rs_send, rs_recv,
           fc_send, fc_recv, ar_send, ar_recv):
    r = lax.axis_index("row")
    c = lax.axis_index("col")
    z = r // 2
    core = lax.rem(r, 2)
    cx = lax.rem(c, SIDE)
    cy = c // SIDE

    for t in range(8):
        pltpu.make_async_copy(tiles_ref.at[pl.ds(4 * t, 4)], stage.at[pl.ds(4 * t, 4)], tile_sem.at[t]).start()

    barrier = pltpu.get_barrier_semaphore()
    for q in range(1, 16):
        pl.semaphore_signal(barrier, inc=1, device_id={"row": lax.rem(r + q, 16)})
        pl.semaphore_signal(barrier, inc=1, device_id={"col": lax.rem(c + q, 16)})

    def slot_of(distance):
        return lax.rem(z - distance + Z, Z) * 2 + core

    def z_copy(a, d, hop, q):
        slot = slot_of((hop - 1) * (1 if d == 0 else -1))
        target = lax.rem(z + (1 if d == 0 else Z - 1), Z) * 2 + core
        piece = xg.at[a, slot, q // 2, pl.ds(16 * (q % 2), 16)]
        return pltpu.make_async_remote_copy(
            src_ref=piece, dst_ref=piece,
            send_sem=z_send.at[a, d, hop - 1, q], recv_sem=z_recv.at[a, d, hop - 1, q],
            device_id={"row": target})

    def p_copy(a, k, h):
        distance = k if k <= 3 else (4 if k == 7 else 3 - k)
        piece = xg.at[a, slot_of(distance), h]
        return pltpu.make_async_remote_copy(
            src_ref=piece, dst_ref=piece,
            send_sem=p_send.at[a, k, h], recv_sem=p_recv.at[a, k, h],
            device_id={"row": r + 1 - 2 * core})

    def convert(a, slot, h):
        high, low = split(xg[a, slot, h])
        xs[slot * 2 + h, 0:32, :] = high
        xs[slot * 2 + h, 32:64, :] = low

    def exists(d, hop, h):
        return hop <= 3 or (hop == 4 and h == d)

    def gather_send(a, h):
        for q in (2 * h, 2 * h + 1):
            for d in range(2):
                z_copy(a, d, 1, q).start()
        p_copy(a, 0, h).start()

    def gather_hop(a, hop):
        for q in range(4):
            h = q // 2
            for d in range(2):
                if exists(d, hop, h):
                    z_copy(a, d, hop, q).wait_recv()
                    if exists(d, hop + 1, h):
                        z_copy(a, d, hop + 1, q).start()
                    if q % 2 == 1:
                        k = 7 if hop == 4 else hop + 3 * d
                        p_copy(a, k, h).start()
                        convert(a, slot_of(hop * (1 if d == 0 else -1)), h)

    def gather_end(a):
        for k in range(8):
            distance = k if k <= 3 else (4 if k == 7 else 3 - k)
            slot = slot_of(distance) + 1 - 2 * core
            for h in range(2):
                p_copy(a, k, h).wait_recv()
                convert(a, slot, h)
        for hop in range(1, 5):
            for q in range(4):
                for d in range(2):
                    if exists(d, hop, q // 2):
                        z_copy(a, d, hop, q).wait_send()
        for k in range(8):
            for h in range(2):
                p_copy(a, k, h).wait_send()

    def products():
        def one(t):
            j = index_ref[0, t]
            both = lax.dot_general(xs[j], whi[t], NN, preferred_element_type=F32)
            cross = lax.dot_general(xs[j, 0:32, :], wlo[t], NN, preferred_element_type=F32)
            run[t] = (both[0:32] + both[32:64]) + cross + run[index_ref[1, t]]

        def group(g, carry):
            for u in range(4):
                one(g * 4 + u)
            return carry
        lax.fori_loop(0, TMAX // 4, group, 0)

    def split_tiles(t):
        def one(i, carry):
            high, low = split(stage[i].T)
            whi[i] = high
            wlo[i] = low
            return carry
        lax.fori_loop(4 * t, 4 * t + 4, one, 0)

    flips = (
        {"col": cy * SIDE + flip_low(cx)},
        {"col": cy * SIDE + flip_high(cx)},
        {"col": flip_low(cy) * SIDE + cx},
        {"col": flip_high(cy) * SIDE + cx},
    )

    def owner(bits):
        px, py = cx, cy
        if bits[0]:
            px = flip_low(px)
        if bits[1]:
            px = flip_high(px)
        if bits[2]:
            py = flip_low(py)
        if bits[3]:
            py = flip_high(py)
        return py * SIDE + px

    def place(s, bits):
        return sum(bits[(s + step) % 4] << (3 - step) for step in range(4))

    combos = [tuple((n >> k) & 1 for k in range(4)) for n in range(16)]

    def pair_bits(s, steps):
        bits = [0, 0, 0, 0]
        for step in steps:
            bits[(s + step) % 4] = 1
        return tuple(bits)

    def scatter_copy(a, s, h, n):
        size = (8, 4, 1, 1, 1)[n]
        first = (8, 4, 2, 1, 3)[n]
        start = (0, 8, 12, 13, 14)[n]
        steps = ((0,), (1,), (2,), (3,), (2, 3))[n]
        return pltpu.make_async_remote_copy(
            src_ref=part.at[a, s, h, pl.ds(first, size)],
            dst_ref=land.at[a, s, h, pl.ds(start, size)],
            send_sem=rs_send.at[a, s, h, n], recv_sem=rs_recv.at[a, s, h, n],
            device_id={"col": owner(pair_bits(s, steps))})

    def scatter_place(a, h, sent):
        for bits in combos:
            block = run[index_ref[2, 2 * owner(bits) + h]]
            for s in range(4):
                if bits[s] == sent:
                    part[a, s, h, place(s, bits)] = block[8 * s : 8 * s + 8, :]

    def scatter(a):
        for h in range(2):
            scatter_place(a, h, 1)
            for s in range(4):
                scatter_copy(a, s, h, 0).start()
        for h in range(2):
            scatter_place(a, h, 0)
        for h in range(2):
            for s in range(4):
                scatter_copy(a, s, h, 0).wait_recv()
                part[a, s, h, 4:8] = part[a, s, h, 4:8] + land[a, s, h, 4:8]
                scatter_copy(a, s, h, 1).start()
                part[a, s, h, 0:4] = part[a, s, h, 0:4] + land[a, s, h, 0:4]
        for h in range(2):
            for s in range(4):
                scatter_copy(a, s, h, 1).wait_recv()
                part[a, s, h, 1:4] = part[a, s, h, 1:4] + land[a, s, h, 9:12]
                for n in (4, 2, 3):
                    scatter_copy(a, s, h, n).start()

    def scatter_sum(a, s, h):
        for n in (2, 3, 4):
            scatter_copy(a, s, h, n).wait_recv()
        own = part[a, s, h, 0] + land[a, s, h, 8]
        return (own + land[a, s, h, 12]) + (land[a, s, h, 13] + land[a, s, h, 14])

    def scatter_end(a):
        for s in range(4):
            for h in range(2):
                for n in range(5):
                    scatter_copy(a, s, h, n).wait_send()

    def fcol_copy(s, step):
        size = 1 << step
        return pltpu.make_async_remote_copy(
            src_ref=fcol.at[s, pl.ds(0, size)],
            dst_ref=fcol.at[s, pl.ds(size, size)],
            send_sem=fc_send.at[s, step], recv_sem=fc_recv.at[s, step],
            device_id=flips[(s + 3 - step) % 4])

    def ar_copy(w, level, q):
        if level == 0:
            mine, peer = r, {"row": lax.rem(r + q, 16)}
        else:
            mine, peer = c, {"col": lax.rem(c + q, 16)}
        piece = red.at[w, level, mine]
        return pltpu.make_async_remote_copy(
            src_ref=piece, dst_ref=piece,
            send_sem=ar_send.at[w, level, q], recv_sem=ar_recv.at[w, level, q],
            device_id=peer)

    def ar_start(w, level, value):
        red[w, level, r if level == 0 else c] = value
        for q in range(1, 16):
            ar_copy(w, level, q).start()

    def ar_end(w, level):
        for q in range(1, 16):
            ar_copy(w, level, q).wait_recv()
        total = red[w, level, 0]
        for q in range(1, 16):
            total = total + red[w, level, q]
        for q in range(1, 16):
            ar_copy(w, level, q).wait_send()
        return total

    for h in range(2):
        xg[0, r, h] = x_ref[:, BS * h : BS * h + BS]
    run[TMAX] = jnp.zeros((SUB, BS), F32)
    pl.semaphore_wait(barrier, 30)
    for h in range(2):
        gather_send(0, h)
    for h in range(2):
        convert(0, r, h)
    for hop in range(1, 5):
        for t in range(2 * hop - 2, 2 * hop):
            pltpu.make_async_copy(tiles_ref.at[pl.ds(4 * t, 4)], stage.at[pl.ds(4 * t, 4)], tile_sem.at[t]).wait()
            split_tiles(t)
        gather_hop(0, hop)
    gather_end(0)

    for a in range(3):
        if a > 0:
            for hop in range(1, 5):
                gather_hop(a, hop)
            gather_end(a)
        products()
        scatter(a)
        for h in range(2):
            gap = deg_ref[0:1, BS * h : BS * h + BS] - CENTER
            for s in range(4):
                rows = slice(8 * s, 8 * s + 8)
                now = xg[a, r, h, rows, :]
                image = (gap * now - scatter_sum(a, s, h)) * INV_RADIUS
                if a > 0:
                    image = 2.0 * image - xg[a - 1, r, h, rows, :]
                xg[a + 1, r, h, rows, :] = image
                if a == 2:
                    fcol[s, 0, h] = image
            gather_send(a + 1, h)
        for h in range(2):
            convert(a + 1, r, h)
        scatter_end(a)

    for s in range(4):
        fcol_copy(s, 0).start()
    gram = jnp.zeros((SUB, SUB), F32)
    shift = jnp.zeros((SUB, SUB), F32)
    for h in range(2):
        own = xg[3, r, h]
        gram = gram + lax.dot_general(own, own, NT, precision=HIGH, preferred_element_type=F32)
        shift = shift + lax.dot_general(own, own * deg_ref[0:1, BS * h : BS * h + BS], NT, precision=HIGH,
                                        preferred_element_type=F32)
    ar_start(0, 0, pack(gram))

    def column_step(step):
        for s in range(4):
            fcol_copy(s, step).wait_recv()
            if step < 3:
                fcol_copy(s, step + 1).start()

    gather_hop(3, 1)
    column_step(0)
    gather_hop(3, 2)
    column_step(1)
    ar_start(0, 1, ar_end(0, 0))
    gather_hop(3, 3)
    column_step(2)
    gather_hop(3, 4)
    gather_end(3)
    products()
    column_step(3)
    for s in range(4):
        for step in range(4):
            fcol_copy(s, step).wait_send()
    quad = jnp.zeros((2 * SUB, 2 * SUB), F32)
    for bits in combos:
        for h in range(2):
            mine = jnp.concatenate([fcol[s, place(s, bits), h] for s in range(4)], axis=0)
            left = jnp.concatenate(split(mine), axis=0)
            right = jnp.concatenate(split(run[index_ref[2, 2 * owner(bits) + h]]), axis=0)
            quad = quad + lax.dot_general(left, right, NT, preferred_element_type=F32)
    coupling = quad[0:32, 0:32] + quad[0:32, 32:64] + quad[32:64, 0:32] + quad[32:64, 32:64]
    ar_start(1, 0, pack(shift - coupling))
    total_gram = unpack(ar_end(0, 1)) * (1.0 / NVERT)
    inv = inverse_factor(total_gram)
    for h in range(2):
        basis_ref[:, BS * h : BS * h + BS] = lax.dot_general(
            inv, xg[3, r, h], NN, precision=HIGH, preferred_element_type=F32)
    ar_start(1, 1, ar_end(1, 0))
    moment = unpack(ar_end(1, 1)) * (1.0 / NVERT)
    half = lax.dot_general(inv, moment, NN, precision=HIGH, preferred_element_type=F32)
    full = lax.dot_general(half, inv, NT, precision=HIGH, preferred_element_type=F32)
    proj_ref[...] = 0.5 * (full + full.T)


def body(start_basis, degrees, tiles, tile_rows, tile_cols, counts):
    rows = tile_rows[0]
    live = counts[0, 0]
    slot = jnp.arange(TMAX, dtype=jnp.int32)
    earlier = (rows[:, None] == rows[None, :]) & (slot[None, :] < slot[:, None])
    before = jnp.max(jnp.where(earlier, slot[None, :], -1), axis=1)
    before = jnp.where(before < 0, TMAX, before)
    ends = (rows[None, :] == slot[:, None]) & (slot[None, :] < live)
    last = jnp.max(jnp.where(ends, slot[None, :], -1), axis=1)
    last = jnp.where(last < 0, TMAX, last)
    index = jnp.stack([tile_cols[0], before, last])
    vmem = pl.BlockSpec(memory_space=pltpu.VMEM)
    dma = pltpu.SemaphoreType.DMA
    return pl.pallas_call(
        kernel,
        out_shape=(jax.ShapeDtypeStruct((SUB, 2 * BS), F32), jax.ShapeDtypeStruct((SUB, SUB), F32)),
        in_specs=[pl.BlockSpec(memory_space=pltpu.SMEM), vmem, vmem, pl.BlockSpec(memory_space=pl.ANY)],
        out_specs=(vmem, vmem),
        scratch_shapes=[
            pltpu.VMEM((TMAX, BS, BS), F32),
            pltpu.VMEM((TMAX, BS, BS), BF16),
            pltpu.VMEM((TMAX, BS, BS), BF16),
            pltpu.VMEM((4, N_ROW, 2, SUB, BS), F32),
            pltpu.VMEM((2 * N_ROW, 2 * SUB, BS), BF16),
            pltpu.VMEM((TMAX + 1, SUB, BS), F32),
            pltpu.VMEM((3, 4, 2, 16, 8, BS), F32),
            pltpu.VMEM((3, 4, 2, 15, 8, BS), F32),
            pltpu.VMEM((4, 16, 2, 8, BS), F32),
            pltpu.VMEM((2, 2, 16, 8, 128), F32),
            dma((8,)),
            dma((4, 2, 4, 4)), dma((4, 2, 4, 4)),
            dma((4, 8, 2)), dma((4, 8, 2)),
            dma((3, 4, 2, 5)), dma((3, 4, 2, 5)),
            dma((4, 4)), dma((4, 4)),
            dma((2, 2, 16)), dma((2, 2, 16)),
        ],
        compiler_params=pltpu.CompilerParams(collective_id=0, has_side_effects=True, vmem_limit_bytes=56 << 20),
        name="subspace_step",
    )(index, start_basis, degrees.reshape(1, -1), tiles)


def solution(mesh):
    return jax.shard_map(
        body,
        mesh=mesh,
        in_specs=(
            P(None, ("row", "col")),
            P(("row", "col")),
            P(("row", "col"), None, None),
            P("row", "col"),
            P("row", "col"),
            P("row", "col"),
        ),
        out_specs=(P(None, ("row", "col")), P()),
        check_vma=False,
    )
```

```python
import jax
import jax.numpy as jnp
from jax import lax
from jax.experimental import pallas as pl
from jax.experimental.pallas import tpu as pltpu
from jax.sharding import PartitionSpec as P

BS = 256
SUB = 32
TMAX = 32
N_ROW = 16
N_COL = 16
SIDE = 4
Z = 8
NVERT = 131072

CENTER = 1.0
INV_RADIUS = 1.0 / 1.4

F32 = jnp.float32
BF16 = jnp.bfloat16
HIGH = lax.Precision.HIGHEST
NT = (((1,), (1,)), ((), ()))
NN = (((1,), (0,)), ((), ()))


def split(value):
    high = value.astype(BF16)
    return high, (value - high.astype(F32)).astype(BF16)


def pack(square):
    return jnp.concatenate([square[8 * s : 8 * s + 8, :] for s in range(4)], axis=1)


def unpack(flat):
    return jnp.concatenate([flat[:, 32 * s : 32 * s + 32] for s in range(4)], axis=0)


def flip_low(p):
    return p + 1 - 2 * lax.rem(p, 2)


def flip_high(p):
    return lax.rem(p + 3 + 2 * lax.rem(p, 2), SIDE)


def inverse_factor(gram):
    rows = lax.broadcasted_iota(jnp.int32, (32, 128), 0)
    lanes = lax.broadcasted_iota(jnp.int32, (32, 128), 1)
    eye = (rows[:, :32] == lanes[:, :32]).astype(F32)
    table = jnp.concatenate([eye, gram, jnp.zeros((32, 64), F32)], axis=1)
    for j in range(32):
        pivot = table[j : j + 1, 32 + j : 33 + j]
        guess = lax.rsqrt(pivot)
        inv = guess * (1.5 - 0.5 * pivot * guess * guess)
        row = table[j : j + 1, :] * inv
        col = table[:, 32 + j : 33 + j] * inv
        table = jnp.where(rows == j, row, jnp.where(rows > j, table - col * row, table))
    return table[:, :32]


def kernel(index_ref, x_ref, deg_ref, tiles_ref, basis_ref, proj_ref,
           stage, whi, wlo, xg, xs, run, part, land, fcol, red,
           tile_sem, z_send, z_recv, p_send, p_recv, rs_send, rs_recv,
           fc_send, fc_recv, ar_send, ar_recv):
    r = lax.axis_index("row")
    c = lax.axis_index("col")
    z = r // 2
    core = lax.rem(r, 2)
    cx = lax.rem(c, SIDE)
    cy = c // SIDE

    for t in range(8):
        pltpu.make_async_copy(tiles_ref.at[pl.ds(4 * t, 4)], stage.at[pl.ds(4 * t, 4)], tile_sem.at[t]).start()

    barrier = pltpu.get_barrier_semaphore()
    for q in range(1, 16):
        pl.semaphore_signal(barrier, inc=1, device_id={"row": lax.rem(r + q, 16)})
        pl.semaphore_signal(barrier, inc=1, device_id={"col": lax.rem(c + q, 16)})

    def slot_of(distance):
        return lax.rem(z - distance + Z, Z) * 2 + core

    def z_copy(a, d, hop, h):
        slot = slot_of((hop - 1) * (1 if d == 0 else -1))
        target = lax.rem(z + (1 if d == 0 else Z - 1), Z) * 2 + core
        piece = xg.at[a, slot, h]
        return pltpu.make_async_remote_copy(
            src_ref=piece, dst_ref=piece,
            send_sem=z_send.at[a, d, hop - 1, h], recv_sem=z_recv.at[a, d, hop - 1, h],
            device_id={"row": target})

    def p_copy(a, k, h):
        distance = k if k <= 3 else (4 if k == 7 else 3 - k)
        piece = xg.at[a, slot_of(distance), h]
        return pltpu.make_async_remote_copy(
            src_ref=piece, dst_ref=piece,
            send_sem=p_send.at[a, k, h], recv_sem=p_recv.at[a, k, h],
            device_id={"row": r + 1 - 2 * core})

    def convert(a, slot, h):
        high, low = split(xg[a, slot, h])
        xs[slot * 2 + h, 0:32, :] = high
        xs[slot * 2 + h, 32:64, :] = low

    def exists(d, hop, h):
        return hop <= 3 or (hop == 4 and h == d)

    def gather_send(a, h):
        for d in range(2):
            z_copy(a, d, 1, h).start()
        p_copy(a, 0, h).start()

    def gather_hop(a, hop):
        for h in range(2):
            for d in range(2):
                if exists(d, hop, h):
                    z_copy(a, d, hop, h).wait_recv()
                    if exists(d, hop + 1, h):
                        z_copy(a, d, hop + 1, h).start()
                    k = 7 if hop == 4 else hop + 3 * d
                    p_copy(a, k, h).start()
                    convert(a, slot_of(hop * (1 if d == 0 else -1)), h)

    def gather_end(a):
        for k in range(8):
            distance = k if k <= 3 else (4 if k == 7 else 3 - k)
            slot = slot_of(distance) + 1 - 2 * core
            for h in range(2):
                p_copy(a, k, h).wait_recv()
                convert(a, slot, h)
        for hop in range(1, 5):
            for h in range(2):
                for d in range(2):
                    if exists(d, hop, h):
                        z_copy(a, d, hop, h).wait_send()
        for k in range(8):
            for h in range(2):
                p_copy(a, k, h).wait_send()

    def products():
        def one(t):
            j = index_ref[0, t]
            both = lax.dot_general(xs[j], whi[t], NN, preferred_element_type=F32)
            cross = lax.dot_general(xs[j, 0:32, :], wlo[t], NN, preferred_element_type=F32)
            run[t] = (both[0:32] + both[32:64]) + cross + run[index_ref[1, t]]

        def group(g, carry):
            for u in range(4):
                one(g * 4 + u)
            return carry
        lax.fori_loop(0, TMAX // 4, group, 0)

    def split_tiles(t):
        def one(i, carry):
            high, low = split(stage[i].T)
            whi[i] = high
            wlo[i] = low
            return carry
        lax.fori_loop(4 * t, 4 * t + 4, one, 0)

    flips = (
        {"col": cy * SIDE + flip_low(cx)},
        {"col": cy * SIDE + flip_high(cx)},
        {"col": flip_low(cy) * SIDE + cx},
        {"col": flip_high(cy) * SIDE + cx},
    )

    def owner(bits):
        px, py = cx, cy
        if bits[0]:
            px = flip_low(px)
        if bits[1]:
            px = flip_high(px)
        if bits[2]:
            py = flip_low(py)
        if bits[3]:
            py = flip_high(py)
        return py * SIDE + px

    def place(s, bits):
        return sum(bits[(s + step) % 4] << (3 - step) for step in range(4))

    combos = [tuple((n >> k) & 1 for k in range(4)) for n in range(16)]

    def pair_bits(s, steps):
        bits = [0, 0, 0, 0]
        for step in steps:
            bits[(s + step) % 4] = 1
        return tuple(bits)

    def scatter_copy(a, s, h, n):
        size = (8, 4, 1, 1, 1)[n]
        first = (8, 4, 2, 1, 3)[n]
        start = (0, 8, 12, 13, 14)[n]
        steps = ((0,), (1,), (2,), (3,), (2, 3))[n]
        return pltpu.make_async_remote_copy(
            src_ref=part.at[a, s, h, pl.ds(first, size)],
            dst_ref=land.at[a, s, h, pl.ds(start, size)],
            send_sem=rs_send.at[a, s, h, n], recv_sem=rs_recv.at[a, s, h, n],
            device_id={"col": owner(pair_bits(s, steps))})

    def scatter_place(a, h, sent):
        for bits in combos:
            block = run[index_ref[2, 2 * owner(bits) + h]]
            for s in range(4):
                if bits[s] == sent:
                    part[a, s, h, place(s, bits)] = block[8 * s : 8 * s + 8, :]

    def scatter(a):
        for h in range(2):
            scatter_place(a, h, 1)
            for s in range(4):
                scatter_copy(a, s, h, 0).start()
        for h in range(2):
            scatter_place(a, h, 0)
        for h in range(2):
            for s in range(4):
                scatter_copy(a, s, h, 0).wait_recv()
                part[a, s, h, 4:8] = part[a, s, h, 4:8] + land[a, s, h, 4:8]
                scatter_copy(a, s, h, 1).start()
                part[a, s, h, 0:4] = part[a, s, h, 0:4] + land[a, s, h, 0:4]
        for h in range(2):
            for s in range(4):
                scatter_copy(a, s, h, 1).wait_recv()
                part[a, s, h, 1:4] = part[a, s, h, 1:4] + land[a, s, h, 9:12]
                for n in (4, 2, 3):
                    scatter_copy(a, s, h, n).start()

    def scatter_sum(a, s, h):
        for n in (2, 3, 4):
            scatter_copy(a, s, h, n).wait_recv()
        own = part[a, s, h, 0] + land[a, s, h, 8]
        return (own + land[a, s, h, 12]) + (land[a, s, h, 13] + land[a, s, h, 14])

    def scatter_end(a):
        for s in range(4):
            for h in range(2):
                for n in range(5):
                    scatter_copy(a, s, h, n).wait_send()

    def fcol_copy(s, step):
        size = 1 << step
        return pltpu.make_async_remote_copy(
            src_ref=fcol.at[s, pl.ds(0, size)],
            dst_ref=fcol.at[s, pl.ds(size, size)],
            send_sem=fc_send.at[s, step], recv_sem=fc_recv.at[s, step],
            device_id=flips[(s + 3 - step) % 4])

    def ar_copy(w, level, q):
        if level == 0:
            mine, peer = r, {"row": lax.rem(r + q, 16)}
        else:
            mine, peer = c, {"col": lax.rem(c + q, 16)}
        piece = red.at[w, level, mine]
        return pltpu.make_async_remote_copy(
            src_ref=piece, dst_ref=piece,
            send_sem=ar_send.at[w, level, q], recv_sem=ar_recv.at[w, level, q],
            device_id=peer)

    def ar_start(w, level, value):
        red[w, level, r if level == 0 else c] = value
        for q in range(1, 16):
            ar_copy(w, level, q).start()

    def ar_end(w, level):
        for q in range(1, 16):
            ar_copy(w, level, q).wait_recv()
        total = red[w, level, 0]
        for q in range(1, 16):
            total = total + red[w, level, q]
        for q in range(1, 16):
            ar_copy(w, level, q).wait_send()
        return total

    for h in range(2):
        xg[0, r, h] = x_ref[:, BS * h : BS * h + BS]
    run[TMAX] = jnp.zeros((SUB, BS), F32)
    pl.semaphore_wait(barrier, 30)
    for h in range(2):
        gather_send(0, h)
    for h in range(2):
        convert(0, r, h)
    for hop in range(1, 5):
        for t in range(2 * hop - 2, 2 * hop):
            pltpu.make_async_copy(tiles_ref.at[pl.ds(4 * t, 4)], stage.at[pl.ds(4 * t, 4)], tile_sem.at[t]).wait()
            split_tiles(t)
        gather_hop(0, hop)
    gather_end(0)

    for a in range(3):
        if a > 0:
            for hop in range(1, 5):
                gather_hop(a, hop)
            gather_end(a)
        products()
        scatter(a)
        for h in range(2):
            gap = deg_ref[0:1, BS * h : BS * h + BS] - CENTER
            for s in range(4):
                rows = slice(8 * s, 8 * s + 8)
                now = xg[a, r, h, rows, :]
                image = (gap * now - scatter_sum(a, s, h)) * INV_RADIUS
                if a > 0:
                    image = 2.0 * image - xg[a - 1, r, h, rows, :]
                xg[a + 1, r, h, rows, :] = image
                if a == 2:
                    fcol[s, 0, h] = image
            gather_send(a + 1, h)
        for h in range(2):
            convert(a + 1, r, h)
        scatter_end(a)

    for s in range(4):
        fcol_copy(s, 0).start()
    gram = jnp.zeros((SUB, SUB), F32)
    shift = jnp.zeros((SUB, SUB), F32)
    for h in range(2):
        own = xg[3, r, h]
        gram = gram + lax.dot_general(own, own, NT, precision=HIGH, preferred_element_type=F32)
        shift = shift + lax.dot_general(own, own * deg_ref[0:1, BS * h : BS * h + BS], NT, precision=HIGH,
                                        preferred_element_type=F32)
    ar_start(0, 0, pack(gram))

    def column_step(step):
        for s in range(4):
            fcol_copy(s, step).wait_recv()
            if step < 3:
                fcol_copy(s, step + 1).start()

    gather_hop(3, 1)
    column_step(0)
    gather_hop(3, 2)
    column_step(1)
    ar_start(0, 1, ar_end(0, 0))
    gather_hop(3, 3)
    column_step(2)
    gather_hop(3, 4)
    gather_end(3)
    products()
    column_step(3)
    for s in range(4):
        for step in range(4):
            fcol_copy(s, step).wait_send()
    quad = jnp.zeros((2 * SUB, 2 * SUB), F32)
    for bits in combos:
        for h in range(2):
            mine = jnp.concatenate([fcol[s, place(s, bits), h] for s in range(4)], axis=0)
            left = jnp.concatenate(split(mine), axis=0)
            right = jnp.concatenate(split(run[index_ref[2, 2 * owner(bits) + h]]), axis=0)
            quad = quad + lax.dot_general(left, right, NT, preferred_element_type=F32)
    coupling = quad[0:32, 0:32] + quad[0:32, 32:64] + quad[32:64, 0:32] + quad[32:64, 32:64]
    ar_start(1, 0, pack(shift - coupling))
    total_gram = unpack(ar_end(0, 1)) * (1.0 / NVERT)
    inv = inverse_factor(total_gram)
    for h in range(2):
        basis_ref[:, BS * h : BS * h + BS] = lax.dot_general(
            inv, xg[3, r, h], NN, precision=HIGH, preferred_element_type=F32)
    ar_start(1, 1, ar_end(1, 0))
    moment = unpack(ar_end(1, 1)) * (1.0 / NVERT)
    half = lax.dot_general(inv, moment, NN, precision=HIGH, preferred_element_type=F32)
    full = lax.dot_general(half, inv, NT, precision=HIGH, preferred_element_type=F32)
    proj_ref[...] = 0.5 * (full + full.T)


def body(start_basis, degrees, tiles, tile_rows, tile_cols, counts):
    rows = tile_rows[0]
    live = counts[0, 0]
    slot = jnp.arange(TMAX, dtype=jnp.int32)
    earlier = (rows[:, None] == rows[None, :]) & (slot[None, :] < slot[:, None])
    before = jnp.max(jnp.where(earlier, slot[None, :], -1), axis=1)
    before = jnp.where(before < 0, TMAX, before)
    ends = (rows[None, :] == slot[:, None]) & (slot[None, :] < live)
    last = jnp.max(jnp.where(ends, slot[None, :], -1), axis=1)
    last = jnp.where(last < 0, TMAX, last)
    index = jnp.stack([tile_cols[0], before, last])
    vmem = pl.BlockSpec(memory_space=pltpu.VMEM)
    dma = pltpu.SemaphoreType.DMA
    return pl.pallas_call(
        kernel,
        out_shape=(jax.ShapeDtypeStruct((SUB, 2 * BS), F32), jax.ShapeDtypeStruct((SUB, SUB), F32)),
        in_specs=[pl.BlockSpec(memory_space=pltpu.SMEM), vmem, vmem, pl.BlockSpec(memory_space=pl.ANY)],
        out_specs=(vmem, vmem),
        scratch_shapes=[
            pltpu.VMEM((TMAX, BS, BS), F32),
            pltpu.VMEM((TMAX, BS, BS), BF16),
            pltpu.VMEM((TMAX, BS, BS), BF16),
            pltpu.VMEM((4, N_ROW, 2, SUB, BS), F32),
            pltpu.VMEM((2 * N_ROW, 2 * SUB, BS), BF16),
            pltpu.VMEM((TMAX + 1, SUB, BS), F32),
            pltpu.VMEM((3, 4, 2, 16, 8, BS), F32),
            pltpu.VMEM((3, 4, 2, 15, 8, BS), F32),
            pltpu.VMEM((4, 16, 2, 8, BS), F32),
            pltpu.VMEM((2, 2, 16, 8, 128), F32),
            dma((8,)),
            dma((4, 2, 4, 2)), dma((4, 2, 4, 2)),
            dma((4, 8, 2)), dma((4, 8, 2)),
            dma((3, 4, 2, 5)), dma((3, 4, 2, 5)),
            dma((4, 4)), dma((4, 4)),
            dma((2, 2, 16)), dma((2, 2, 16)),
        ],
        compiler_params=pltpu.CompilerParams(collective_id=0, has_side_effects=True, vmem_limit_bytes=56 << 20),
        name="subspace_step",
    )(index, start_basis, degrees.reshape(1, -1), tiles)


def solution(mesh):
    return jax.shard_map(
        body,
        mesh=mesh,
        in_specs=(
            P(None, ("row", "col")),
            P(("row", "col")),
            P(("row", "col"), None, None),
            P("row", "col"),
            P("row", "col"),
            P("row", "col"),
        ),
        out_specs=(P(None, ("row", "col")), P()),
        check_vma=False,
    )
```
